1024 devices in a mesh: dp: 32 (over z, core), space: 32 (over x, y).
Axes of the slice: x: 4, y: 8, z: 16, core: 2. Of those that a mesh axis runs over, the one named last changes fastest.
Arguments:
- cotangent: bfloat16 [32, 24, 1024, 1024], P('dp', None, 'space'), may hold values from -6 to 6
- spectrum: float32 [64, 32, 24, 128], P('space', 'dp'), may hold values from -6 to 6
- weights: float32 [64, 24, 24, 128], P('space'), may hold values from -0.875 to 0.875
Outputs:
- grad_input: bfloat16 [32, 24, 1024, 1024], P('dp', None, 'space')
- grad_weights: float32 [64, 576, 128], P('space', 'dp')
The draws below stay inside these ranges and needn't reach their ends.
All inputs are finite; a program needn't handle non-finite values.
Results may differ from the reference program's by a relative error of at most 0.001.
Values sent between devices are 32-bit elements; how exact they have to be, the bound alone decides.
No kernel may reach another device: no remote copies, remote signals or barrier semaphores. Data moves between devices by JAX's collectives and lax.ppermute only.
A program may use at most 32 MiB of HBM per device.

```python
import math
import jax
import jax.numpy as jnp
from jax import lax

C = 24
M1 = 64
M2 = 64
W = 1024
H = 1024
BATCH = 32


def levels(stream_key, shape, split, low, top_value):
    def one(axis_at, shards_of):
        steps = jax.random.uniform(jax.random.fold_in(jax.random.fold_in(stream_key, 6), axis_at), (shards_of,), jnp.float32, low / len(split), top_value / len(split))
        return jnp.repeat(jnp.exp(steps), shape[axis_at] // shards_of).reshape((-1,) + (1,) * (len(shape) - axis_at - 1))

    loudness = one(*split[0])
    for cut in split[1:]:
        loudness = loudness * one(*cut)
    return loudness


def scatter_about(own_key, dims, scale, bound, shards=(), held_as=jnp.bfloat16):
    values = scale * jax.random.normal(own_key, dims, jnp.float32)
    if shards:
        values = values * levels(own_key, dims, shards, -0.22, 0.18)
    return jnp.clip(values, -bound, bound).astype(held_as)


def setup_inputs(seed: int = 0) -> dict:
    streams_of = jax.random.split(jax.random.key(seed), 4)
    cotangent = scatter_about(streams_of[0], (BATCH, C, H, W), 1.0, 6.0, ((0, 32), (2, 32)))
    spectrum = scatter_about(streams_of[1], (M1, BATCH, C, 2 * M2), 1.0, 6.0, ((0, 32), (1, 32)), jnp.float32)
    weights = scatter_about(streams_of[2], (M1, C, C, 2 * M2), (2 * C) ** -0.5, 0.875, ((0, 32),), jnp.float32)
    return dict(cotangent=cotangent, spectrum=spectrum, weights=weights)


def column_basis(col_count, modes_y):
    position = jnp.arange(col_count, dtype=jnp.int32)
    frequency = jnp.arange(modes_y, dtype=jnp.int32)
    phase = position[:, None] * frequency[None, :] % col_count
    angles = phase.astype(jnp.float32) * (2.0 * math.pi / col_count)
    return jnp.concatenate([jnp.cos(angles), -jnp.sin(angles)], axis=1)

def row_basis(first_mode, mode_count, first_row, row_count, height):
    frequency = first_mode + jnp.arange(mode_count, dtype=jnp.int32)
    position = first_row + jnp.arange(row_count, dtype=jnp.int32)
    phase = frequency[:, None] * position[None, :] % height
    angles = phase.astype(jnp.float32) * (2.0 * math.pi / height)
    return (jnp.cos(angles), jnp.sin(angles))

def spectral_backward(spec_grad, weights, modes_y):
    hp = lax.Precision.HIGHEST
    grad_re, grad_im = (spec_grad[..., :modes_y], spec_grad[..., modes_y:])
    weight_re, weight_im = (weights[..., :modes_y], weights[..., modes_y:])
    real_part = jnp.einsum('kbox,kcox->kbcx', grad_re, weight_re, precision=hp) + jnp.einsum('kbox,kcox->kbcx', grad_im, weight_im, precision=hp)
    imag_part = jnp.einsum('kbox,kcox->kbcx', grad_im, weight_re, precision=hp) - jnp.einsum('kbox,kcox->kbcx', grad_re, weight_im, precision=hp)
    return jnp.concatenate([real_part, imag_part], axis=-1)

def weight_terms(spectrum, spec_grad, modes_y):
    hp = lax.Precision.HIGHEST
    spec_re, spec_im = (spectrum[..., :modes_y], spectrum[..., modes_y:])
    grad_re, grad_im = (spec_grad[..., :modes_y], spec_grad[..., modes_y:])
    real_part = jnp.einsum('kbcx,kbox->kcox', spec_re, grad_re, precision=hp) + jnp.einsum('kbcx,kbox->kcox', spec_im, grad_im, precision=hp)
    imag_part = jnp.einsum('kbcx,kbox->kcox', spec_re, grad_im, precision=hp) - jnp.einsum('kbcx,kbox->kcox', spec_im, grad_re, precision=hp)
    joined = jnp.concatenate([real_part, imag_part], axis=-1)
    return joined.reshape(joined.shape[0], joined.shape[1] * joined.shape[2], joined.shape[3])

def reference(cotangent, spectrum, weights):
    hp = lax.Precision.HIGHEST
    basis = column_basis(W, M2)

    def column_pass(raster):
        return jnp.einsum('cxw,wj->cxj', raster.astype(jnp.float32), basis, precision=hp)
    col_spec = lax.map(column_pass, cotangent)
    cosines, sines = row_basis(0, M1, 0, H, H)
    forward_scale = 1.0 / math.sqrt(H * W)
    with_cos = jnp.einsum('kx,bcxj->kbcj', cosines, col_spec, precision=hp)
    with_sin = jnp.einsum('kx,bcxj->kbcj', sines, col_spec, precision=hp)
    spec_grad = jnp.concatenate([with_cos[..., :M2] + with_sin[..., M2:], with_cos[..., M2:] - with_sin[..., :M2]], axis=-1) * forward_scale
    input_spec = spectral_backward(spec_grad, weights, M2)
    grad_weights = weight_terms(spectrum, spec_grad, M2)
    back_cos = jnp.einsum('kx,kbcj->bcxj', cosines, input_spec, precision=hp)
    back_sin = jnp.einsum('kx,kbcj->bcxj', sines, input_spec, precision=hp)
    back = jnp.concatenate([back_cos[..., :M2] - back_sin[..., M2:], back_cos[..., M2:] + back_sin[..., :M2]], axis=-1)
    inverse_scale = 1.0 / math.sqrt(M1 * M2)

    def inverse_pass(block):
        return (jnp.einsum('cxj,wj->cxw', block, basis, precision=hp) * inverse_scale).astype(jnp.bfloat16)
    grad_input = lax.map(inverse_pass, back)
    return (grad_input, grad_weights)
```

```python
import math

import jax
import jax.numpy as jnp
import numpy as np
from jax import lax
from jax.sharding import PartitionSpec as P

HP = lax.Precision.HIGHEST


def column_basis(col_count, modes_y):
    phase = np.arange(col_count)[:, None] * np.arange(modes_y)[None, :] % col_count
    angles = phase * (2.0 * math.pi / col_count)
    return np.concatenate([np.cos(angles), -np.sin(angles)], axis=1).astype(np.float32)


def row_basis(mode_count, first_row, row_count, height):
    frequency = jnp.arange(mode_count, dtype=jnp.int32)
    position = first_row + jnp.arange(row_count, dtype=jnp.int32)
    phase = frequency[:, None] * position[None, :] % height
    angles = phase.astype(jnp.float32) * (2.0 * math.pi / height)
    return (jnp.cos(angles), jnp.sin(angles))


def input_spectrum(spec_grad, weights, modes_y):
    grad_re, grad_im = spec_grad[..., :modes_y], spec_grad[..., modes_y:]
    weight_re, weight_im = weights[..., :modes_y], weights[..., modes_y:]
    re, im = grad_re[:, None], grad_im[:, None]
    real_part = jnp.sum(re * weight_re + im * weight_im, axis=2)
    imag_part = jnp.sum(im * weight_re - re * weight_im, axis=2)
    return jnp.concatenate([real_part, imag_part], axis=-1)


def to_points(spectrum, owners, modes_y):
    modes, channels, _ = spectrum.shape
    split = spectrum.reshape(modes, channels, 2, owners, modes_y // owners)
    return split.transpose(3, 0, 4, 2, 1).reshape(owners, -1, 2 * channels)


def weight_gradient(spectrum_points, grad_points, channels):
    spec_re, spec_im = spectrum_points[..., :channels], spectrum_points[..., channels:]
    grad_re, grad_im = grad_points[..., :channels], grad_points[..., channels:]

    def product(a, b):
        return jnp.einsum("bpc,bpo->pco", a, b, precision=HP)

    real_part = product(spec_re, grad_re) + product(spec_im, grad_im)
    imag_part = product(spec_re, grad_im) - product(spec_im, grad_re)
    return jnp.stack([real_part, imag_part], axis=1)


def body(cotangent, spectrum, weights):
    space_count, dp_count = lax.axis_size("space"), lax.axis_size("dp")
    _, channels, row_count, col_count = cotangent.shape
    local_modes, modes_y = spectrum.shape[0], spectrum.shape[3] // 2
    height, modes_x = row_count * space_count, local_modes * space_count
    basis = jnp.asarray(column_basis(col_count, modes_y))
    first_row = lax.axis_index("space") * row_count
    cosines, sines = row_basis(modes_x, first_row, row_count, height)

    spectrum_points = lax.all_to_all(
        to_points(spectrum[:, 0], dp_count, modes_y), "dp", 0, 0, tiled=True
    )

    col_spec = jnp.einsum(
        "cxw,wj->cxj", cotangent[0], basis, precision=HP, preferred_element_type=jnp.float32
    )
    with_cos = jnp.einsum("kx,cxj->kcj", cosines, col_spec, precision=HP)
    with_sin = jnp.einsum("kx,cxj->kcj", sines, col_spec, precision=HP)
    partial = jnp.concatenate(
        [
            with_cos[..., :modes_y] + with_sin[..., modes_y:],
            with_cos[..., modes_y:] - with_sin[..., :modes_y],
        ],
        axis=-1,
    ) * (1.0 / math.sqrt(height * col_count))
    partial = lax.all_to_all(partial, "space", 0, 0, tiled=True)
    spec_grad = jnp.sum(partial.reshape(space_count, local_modes, channels, 2 * modes_y), axis=0)

    input_spec = input_spectrum(spec_grad, weights, modes_y)
    everyone = jnp.broadcast_to(input_spec[None], (space_count,) + input_spec.shape)
    all_spec = lax.all_to_all(everyone, "space", 0, 0, tiled=True)
    all_spec = all_spec.reshape(modes_x, channels, 2 * modes_y)

    grad_points = lax.all_to_all(to_points(spec_grad, dp_count, modes_y), "dp", 0, 0, tiled=True)
    terms = weight_gradient(spectrum_points, grad_points, channels)
    pairs = channels * channels // dp_count
    terms = terms.reshape(-1, dp_count, pairs).transpose(1, 0, 2)
    terms = lax.all_to_all(terms, "dp", 0, 0, tiled=True)
    terms = terms.reshape(dp_count, local_modes, modes_y // dp_count, 2, pairs)
    grad_weights = terms.transpose(1, 4, 3, 0, 2).reshape(local_modes, pairs, 2 * modes_y)

    back_cos = jnp.einsum("kx,kcj->cxj", cosines, all_spec, precision=HP)
    back_sin = jnp.einsum("kx,kcj->cxj", sines, all_spec, precision=HP)
    back = jnp.concatenate(
        [
            back_cos[..., :modes_y] - back_sin[..., modes_y:],
            back_cos[..., modes_y:] + back_sin[..., :modes_y],
        ],
        axis=-1,
    )
    inverse_scale = 1.0 / math.sqrt(modes_x * modes_y)
    grad_input = jnp.einsum("cxj,wj->cxw", back, basis, precision=HP) * inverse_scale
    return (grad_input.astype(jnp.bfloat16)[None], grad_weights)


def solution(mesh):
    return jax.shard_map(
        body,
        mesh=mesh,
        in_specs=(
            P("dp", None, "space", None),
            P("space", "dp", None, None),
            P("space", None, None, None),
        ),
        out_specs=(P("dp", None, "space", None), P("space", "dp", None)),
        check_vma=False,
    )
```

```python
import math

import jax
import jax.numpy as jnp
import numpy as np
from jax import lax
from jax.sharding import PartitionSpec as P

HP = lax.Precision.HIGHEST


def column_basis(col_count, modes_y):
    phase = np.arange(col_count)[:, None] * np.arange(modes_y)[None, :] % col_count
    angles = phase * (2.0 * math.pi / col_count)
    return np.concatenate([np.cos(angles), -np.sin(angles)], axis=1).astype(np.float32)


def row_basis(mode_count, first_row, row_count, height):
    frequency = jnp.arange(mode_count, dtype=jnp.int32)
    position = first_row + jnp.arange(row_count, dtype=jnp.int32)
    phase = frequency[:, None] * position[None, :] % height
    angles = phase.astype(jnp.float32) * (2.0 * math.pi / height)
    return (jnp.cos(angles), jnp.sin(angles))


def input_spectrum(spec_grad, weights, modes_y):
    grad_re, grad_im = spec_grad[..., :modes_y], spec_grad[..., modes_y:]
    weight_re, weight_im = weights[..., :modes_y], weights[..., modes_y:]
    re, im = grad_re[:, None], grad_im[:, None]
    real_part = jnp.sum(re * weight_re + im * weight_im, axis=2)
    imag_part = jnp.sum(im * weight_re - re * weight_im, axis=2)
    return jnp.concatenate([real_part, imag_part], axis=-1)


def weight_terms(spectrum, spec_grad, modes_y, owners):
    modes, channels, _ = spectrum.shape
    spec_re, spec_im = spectrum[:, :, None, :modes_y], spectrum[:, :, None, modes_y:]
    grad_re, grad_im = spec_grad[:, None, :, :modes_y], spec_grad[:, None, :, modes_y:]
    real_part = spec_re * grad_re + spec_im * grad_im
    imag_part = spec_re * grad_im - spec_im * grad_re
    terms = jnp.concatenate([real_part, imag_part], axis=-1)
    pairs = channels * channels // owners
    terms = terms.reshape(modes, owners, pairs, 2 * modes_y).transpose(1, 0, 2, 3)
    return terms.reshape(owners, modes * pairs, 2 * modes_y)


def shift_dp(x, hop, chips):
    pairs = [(2 * z + c, 2 * ((z + hop) % chips) + c) for z in range(chips) for c in range(2)]
    return lax.ppermute(x, "dp", pairs)


def sum_to_owners(terms, chips):
    index = lax.axis_index("dp")
    core, z = index % 2, index // 2
    by_core = terms.reshape((chips, 2) + terms.shape[1:])
    mine = lax.dynamic_index_in_dim(by_core, core, 1, keepdims=False)
    other = lax.dynamic_index_in_dim(by_core, 1 - core, 1, keepdims=False)
    mine = mine + lax.ppermute(other, "dp", [(i, i ^ 1) for i in range(2 * chips)])
    ahead = lax.dynamic_slice_in_dim(jnp.concatenate([mine, mine]), z, chips)
    groups = ahead.reshape((chips // 4, 4) + ahead.shape[1:])
    near = groups[:, 0]
    behind = jnp.concatenate([groups[-1:, 3], groups[:-1, 3]])
    for part, hop in ((groups[:, 1], 1), (behind, -1), (groups[:, 2], 2)):
        near = near + shift_dp(part, hop, chips)
    total = near[0]
    for step in range(1, chips // 4):
        total = total + shift_dp(near[step], 4 * step, chips)
    return total


def body(cotangent, spectrum, weights):
    space_count, dp_count = lax.axis_size("space"), lax.axis_size("dp")
    _, channels, row_count, col_count = cotangent.shape
    local_modes, modes_y = spectrum.shape[0], spectrum.shape[3] // 2
    height, modes_x = row_count * space_count, local_modes * space_count
    basis = jnp.asarray(column_basis(col_count, modes_y))
    first_row = lax.axis_index("space") * row_count
    cosines, sines = row_basis(modes_x, first_row, row_count, height)

    col_spec = jnp.einsum(
        "cxw,wj->cxj", cotangent[0], basis, precision=HP, preferred_element_type=jnp.float32
    )
    with_cos = jnp.einsum("kx,cxj->kcj", cosines, col_spec, precision=HP)
    with_sin = jnp.einsum("kx,cxj->kcj", sines, col_spec, precision=HP)
    partial = jnp.concatenate(
        [
            with_cos[..., :modes_y] + with_sin[..., modes_y:],
            with_cos[..., modes_y:] - with_sin[..., :modes_y],
        ],
        axis=-1,
    ) * (1.0 / math.sqrt(height * col_count))
    partial = lax.all_to_all(partial, "space", 0, 0, tiled=True)
    spec_grad = jnp.sum(partial.reshape(space_count, local_modes, channels, 2 * modes_y), axis=0)

    input_spec = input_spectrum(spec_grad, weights, modes_y)
    everyone = jnp.broadcast_to(input_spec[None], (space_count,) + input_spec.shape)
    all_spec = lax.all_to_all(everyone, "space", 0, 0, tiled=True)
    all_spec = all_spec.reshape(modes_x, channels, 2 * modes_y)

    terms = weight_terms(spectrum[:, 0], spec_grad, modes_y, dp_count)
    grad_weights = sum_to_owners(terms, dp_count // 2).reshape(local_modes, -1, 2 * modes_y)

    back_cos = jnp.einsum("kx,kcj->cxj", cosines, all_spec, precision=HP)
    back_sin = jnp.einsum("kx,kcj->cxj", sines, all_spec, precision=HP)
    back = jnp.concatenate(
        [
            back_cos[..., :modes_y] - back_sin[..., modes_y:],
            back_cos[..., modes_y:] + back_sin[..., :modes_y],
        ],
        axis=-1,
    )
    inverse_scale = 1.0 / math.sqrt(modes_x * modes_y)
    grad_input = jnp.einsum("cxj,wj->cxw", back, basis, precision=HP) * inverse_scale
    return (grad_input.astype(jnp.bfloat16)[None], grad_weights)


def solution(mesh):
    return jax.shard_map(
        body,
        mesh=mesh,
        in_specs=(
            P("dp", None, "space", None),
            P("space", "dp", None, None),
            P("space", None, None, None),
        ),
        out_specs=(P("dp", None, "space", None), P("space", "dp", None)),
        check_vma=False,
    )
```

```python
import math

import jax
import jax.numpy as jnp
import numpy as np
from jax import lax
from jax.sharding import Mesh
from jax.sharding import PartitionSpec as P

HP = lax.Precision.HIGHEST
DP = ("far", "near", "core")


def column_basis(col_count, modes_y):
    phase = np.arange(col_count)[:, None] * np.arange(modes_y)[None, :] % col_count
    angles = phase * (2.0 * math.pi / col_count)
    return np.concatenate([np.cos(angles), -np.sin(angles)], axis=1).astype(np.float32)


def row_basis(mode_count, first_row, row_count, height):
    frequency = jnp.arange(mode_count, dtype=jnp.int32)
    position = first_row + jnp.arange(row_count, dtype=jnp.int32)
    phase = frequency[:, None] * position[None, :] % height
    angles = phase.astype(jnp.float32) * (2.0 * math.pi / height)
    return (jnp.cos(angles), jnp.sin(angles))


def input_spectrum(spec_grad, weights, modes_y):
    grad_re, grad_im = spec_grad[..., :modes_y], spec_grad[..., modes_y:]
    weight_re, weight_im = weights[..., :modes_y], weights[..., modes_y:]
    re, im = grad_re[:, None], grad_im[:, None]
    real_part = jnp.sum(re * weight_re + im * weight_im, axis=2)
    imag_part = jnp.sum(im * weight_re - re * weight_im, axis=2)
    return jnp.concatenate([real_part, imag_part], axis=-1)


def weight_terms(spectrum, spec_grad, modes_y, owners):
    modes, channels, _ = spectrum.shape
    spec_re, spec_im = spectrum[:, :, None, :modes_y], spectrum[:, :, None, modes_y:]
    grad_re, grad_im = spec_grad[:, None, :, :modes_y], spec_grad[:, None, :, modes_y:]
    real_part = spec_re * grad_re + spec_im * grad_im
    imag_part = spec_re * grad_im - spec_im * grad_re
    terms = jnp.concatenate([real_part, imag_part], axis=-1)
    pairs = channels * channels // owners
    terms = terms.reshape(modes, owners, pairs, 2 * modes_y).transpose(1, 0, 2, 3)
    return terms.reshape(owners, modes * pairs, 2 * modes_y)


def shift_near(x, hop):
    near, far = lax.axis_size("near"), lax.axis_size("far")
    chips = near * far
    return lax.ppermute(x, ("far", "near"), [(z, (z + hop) % chips) for z in range(chips)])


def sum_to_owners(terms, later):
    near, far = lax.axis_size("near"), lax.axis_size("far")
    core, here = lax.axis_index("core"), lax.axis_index("near")
    by_core = terms.reshape((far, near, 2) + terms.shape[1:])
    mine = lax.dynamic_index_in_dim(by_core, core, 2, keepdims=False)
    other = lax.dynamic_index_in_dim(by_core, 1 - core, 2, keepdims=False)
    mine = mine + lax.ppermute(other, "core", [(0, 1), (1, 0)])
    ahead = lax.dynamic_slice_in_dim(jnp.concatenate([mine, mine], axis=1), here, near, axis=1)
    total = ahead[:, 0]
    for part, hop in ((ahead[:, 1], 1), (ahead[:, near - 1], -1), (ahead[:, 2], 2)):
        total = total + shift_near(part, hop)
    total, _ = lax.optimization_barrier((total, later))
    return jnp.sum(lax.all_to_all(total, "far", 0, 0, tiled=True), axis=0)


def body(cotangent, spectrum, weights):
    space_count, dp_count = lax.axis_size("space"), lax.axis_size(DP)
    _, channels, row_count, col_count = cotangent.shape
    local_modes, modes_y = spectrum.shape[0], spectrum.shape[3] // 2
    height, modes_x = row_count * space_count, local_modes * space_count
    basis = jnp.asarray(column_basis(col_count, modes_y))
    first_row = lax.axis_index("space") * row_count
    cosines, sines = row_basis(modes_x, first_row, row_count, height)

    col_spec = jnp.einsum(
        "cxw,wj->cxj", cotangent[0], basis, precision=HP, preferred_element_type=jnp.float32
    )
    with_cos = jnp.einsum("kx,cxj->kcj", cosines, col_spec, precision=HP)
    with_sin = jnp.einsum("kx,cxj->kcj", sines, col_spec, precision=HP)
    partial = jnp.concatenate(
        [
            with_cos[..., :modes_y] + with_sin[..., modes_y:],
            with_cos[..., modes_y:] - with_sin[..., :modes_y],
        ],
        axis=-1,
    ) * (1.0 / math.sqrt(height * col_count))
    partial = lax.all_to_all(partial, "space", 0, 0, tiled=True)
    spec_grad = jnp.sum(partial.reshape(space_count, local_modes, channels, 2 * modes_y), axis=0)

    input_spec = input_spectrum(spec_grad, weights, modes_y)
    everyone = jnp.broadcast_to(input_spec[None], (space_count,) + input_spec.shape)
    all_spec = lax.all_to_all(everyone, "space", 0, 0, tiled=True)
    all_spec = all_spec.reshape(modes_x, channels, 2 * modes_y)

    terms = weight_terms(spectrum[:, 0], spec_grad, modes_y, dp_count)
    grad_weights = sum_to_owners(terms, all_spec).reshape(local_modes, -1, 2 * modes_y)

    back_cos = jnp.einsum("kx,kcj->cxj", cosines, all_spec, precision=HP)
    back_sin = jnp.einsum("kx,kcj->cxj", sines, all_spec, precision=HP)
    back = jnp.concatenate(
        [
            back_cos[..., :modes_y] - back_sin[..., modes_y:],
            back_cos[..., modes_y:] + back_sin[..., :modes_y],
        ],
        axis=-1,
    )
    inverse_scale = 1.0 / math.sqrt(modes_x * modes_y)
    grad_input = jnp.einsum("cxj,wj->cxw", back, basis, precision=HP) * inverse_scale
    return (grad_input.astype(jnp.bfloat16)[None], grad_weights)


def solution(mesh):
    dp_count, space_count = mesh.devices.shape
    chips = mesh.devices.reshape(dp_count // 8, 4, 2, space_count)
    return jax.shard_map(
        body,
        mesh=Mesh(chips, DP + ("space",)),
        in_specs=(P(DP, None, "space", None), P("space", DP, None, None), P("space", None, None, None)),
        out_specs=(P(DP, None, "space", None), P("space", DP, None)),
        check_vma=False,
    )
```

```python
import functools
import math

import jax
import jax.numpy as jnp
import ml_dtypes
import numpy as np
from jax import lax
from jax.experimental import pallas as pl
from jax.experimental.pallas import tpu as pltpu
from jax.sharding import Mesh
from jax.sharding import PartitionSpec as P

DP = ("far", "near", "core")
FAR = 4
VMEM = pl.BlockSpec(memory_space=pltpu.VMEM)
SMEM = pl.BlockSpec(memory_space=pltpu.SMEM)
PARAMS = pltpu.CompilerParams(vmem_limit_bytes=24 << 20)


def halves(table):
    high = table.astype(ml_dtypes.bfloat16)
    low = (table - high.astype(np.float64)).astype(ml_dtypes.bfloat16)
    return high, low


def column_table(col_count, modes_y):
    phase = np.arange(col_count)[:, None] * np.arange(modes_y)[None, :] % col_count
    angles = phase * (2.0 * math.pi / col_count)
    return np.concatenate([np.cos(angles), -np.sin(angles)], axis=1)


def row_tables(modes_x, row_count, height):
    phase = np.arange(modes_x)[:, None] * np.arange(height)[None, :] % height
    angles = phase * (2.0 * math.pi / height)
    angles = angles.reshape(modes_x, height // row_count, row_count).transpose(1, 0, 2)
    return np.cos(angles), np.sin(angles)


def split(x):
    high = x.astype(jnp.bfloat16)
    return high, (x - high.astype(jnp.float32)).astype(jnp.bfloat16)


def dot(a, b):
    return jnp.dot(a, b, preferred_element_type=jnp.float32)


def first_half(x, modes_y):
    return lax.broadcasted_iota(jnp.int32, x.shape, x.ndim - 1) < modes_y


def mix(rows, spec, turned):
    high, low = zip(*map(split, spec))
    turned_high, turned_low = zip(*map(split, turned))

    def operand(c):
        return jnp.concatenate(
            [high[c], turned_high[c], low[c], turned_low[c], high[c], turned_high[c]], axis=0
        )

    out, width = [], spec[0].shape[1]
    for c in range(0, len(spec), 2):
        pair = dot(rows, jnp.concatenate([operand(c), operand(c + 1)], axis=1))
        out += [pair[:, :width], pair[:, width:]]
    return out


def forward_kernel(cot_ref, basis_ref, rows_ref, out_ref):
    channels, row_count, col_count = cot_ref.shape
    width = out_ref.shape[2]
    both = dot(cot_ref[...].reshape(channels * row_count, col_count), basis_ref[...])
    col_spec = both[:, :width] + both[:, width:]
    turned = pltpu.roll(col_spec, width // 2, 1)
    turned = jnp.where(first_half(turned, width // 2), turned, -turned)
    parts = [slice(c * row_count, (c + 1) * row_count) for c in range(channels)]
    for c, out in enumerate(mix(rows_ref[...], [col_spec[p] for p in parts], [turned[p] for p in parts])):
        out_ref[:, c, :] = out


def forward(cotangent, block, modes_x, modes_y, height):
    channels, row_count, col_count = cotangent.shape
    basis = np.concatenate(halves(column_table(col_count, modes_y)), axis=1)
    table = np.concatenate(row_tables(modes_x, row_count, height), axis=2) / math.sqrt(height * col_count)
    high, low = halves(table)
    rows = np.concatenate([high, high, low], axis=2)
    rows = lax.dynamic_index_in_dim(jnp.asarray(rows), block, 0, keepdims=False)
    return pl.pallas_call(
        forward_kernel,
        out_shape=jax.ShapeDtypeStruct((modes_x, channels, 2 * modes_y), jnp.float32),
        in_specs=[VMEM, VMEM, VMEM],
        out_specs=VMEM,
        compiler_params=PARAMS,
        name="rows_to_modes",
    )(cotangent, jnp.asarray(basis), rows)


def inverse_kernel(spec_ref, rows_ref, basis_ref, out_ref):
    step, width = out_ref.shape[0], spec_ref.shape[2]
    first = pl.program_id(0) * step
    spec = [spec_ref[first + c] for c in range(step)]
    turned = [pltpu.roll(s, width // 2, 1) for s in spec]
    turned = [jnp.where(first_half(t, width // 2), -t, t) for t in turned]
    high, low = split(jnp.concatenate(mix(rows_ref[...], spec, turned), axis=0))
    raster = dot(jnp.concatenate([high, low, high], axis=1), basis_ref[...])
    out_ref[...] = raster.astype(out_ref.dtype).reshape(out_ref.shape)


def inverse(all_spec, block, row_count, col_count, height):
    channels, modes_x, width = all_spec.shape
    modes_y = width // 2
    high, low = halves(column_table(col_count, modes_y).T)
    basis = np.concatenate([high, high, low], axis=0)
    table = np.concatenate(row_tables(modes_x, row_count, height), axis=1) / math.sqrt(modes_x * modes_y)
    high, low = halves(table.transpose(0, 2, 1))
    rows = np.concatenate([high, high, low], axis=2)
    rows = lax.dynamic_index_in_dim(jnp.asarray(rows), block, 0, keepdims=False)
    step = 8
    return pl.pallas_call(
        inverse_kernel,
        grid=(channels // step,),
        out_shape=jax.ShapeDtypeStruct((channels, row_count, col_count), jnp.bfloat16),
        in_specs=[VMEM, VMEM, VMEM],
        out_specs=pl.BlockSpec((step, row_count, col_count), lambda i: (i, 0, 0)),
        compiler_params=PARAMS,
        name="modes_to_rows",
    )(all_spec, rows, jnp.asarray(basis))


def middle_kernel(got_ref, weights_ref, spectrum_ref, spec_ref, mine_ref, other_ref, one_ref, terms_ref):
    modes, channels, width = spectrum_ref.shape
    sources, near = spec_ref.shape[0], mine_ref.shape[0]
    half = width // 2
    here, core = lax.axis_index("near"), lax.axis_index("core")
    grad = got_ref[pl.ds(0, modes)]
    for s in range(1, sources):
        grad = grad + got_ref[pl.ds(s * modes, modes)]
    turned = pltpu.roll(grad, half, 2)

    for k in range(modes):
        straight, crossed = [], []
        for c in range(channels):
            weight = weights_ref[k, c]
            straight.append(jnp.sum(weight * grad[k], axis=0, keepdims=True))
            crossed.append(jnp.sum(weight * turned[k], axis=0, keepdims=True))
        straight = jnp.concatenate(straight, axis=0)
        crossed = jnp.concatenate(crossed, axis=0)
        left = first_half(straight, half)
        real_part = straight + pltpu.roll(straight, half, 1)
        imag_part = pltpu.roll(crossed, half, 1) - crossed
        one_ref[pl.ds(k, channels, stride=modes), :] = jnp.where(left, real_part, imag_part)
    one = one_ref[...]
    for s in range(sources):
        spec_ref[s] = one

    for k in range(modes):
        own = spectrum_ref[k]
        left = first_half(own, half)
        flipped = pltpu.roll(own, half, 1)
        own_re = jnp.where(left, own, flipped)
        own_im = jnp.where(left, flipped, -own)
        for c in range(channels):
            terms_ref[k, c * channels : (c + 1) * channels] = (
                own_re[c : c + 1] * grad[k] + own_im[c : c + 1] * turned[k]
            )
    rows = mine_ref.shape[1] // FAR
    pairs = rows // modes
    for far in range(FAR):
        for chip in range(near):
            ahead = lax.rem(chip - here + near, near)
            first = 2 * (far * near + chip) * pairs
            for k in range(modes):
                zero = terms_ref[k, first : first + pairs]
                one = terms_ref[k, first + pairs : first + 2 * pairs]
                to = slice(far * rows + k * pairs, far * rows + (k + 1) * pairs)
                mine_ref[ahead, to] = jnp.where(core == 0, zero, one)
                other_ref[ahead, to] = jnp.where(core == 0, one, zero)


def middle(got, weights, spectrum):
    modes, channels, width = spectrum.shape
    sources, near = got.shape[0] // modes, lax.axis_size("near")
    owners = channels * channels * modes // (2 * near)
    terms = jax.ShapeDtypeStruct((near, owners, width), jnp.float32)
    return pl.pallas_call(
        middle_kernel,
        out_shape=(jax.ShapeDtypeStruct((sources, channels * modes, width), jnp.float32), terms, terms),
        in_specs=[VMEM, VMEM, VMEM],
        out_specs=(VMEM, VMEM, VMEM),
        scratch_shapes=[
            pltpu.VMEM((channels * modes, width), jnp.float32),
            pltpu.VMEM((modes, channels * channels, width), jnp.float32),
        ],
        compiler_params=PARAMS,
        name="modes",
    )(got, weights, spectrum)


def shift_near(x, hop):
    near, far = lax.axis_size("near"), lax.axis_size("far")
    chips = near * far
    return lax.ppermute(x, ("far", "near"), [(z, (z + hop) % chips) for z in range(chips)])


def sum_to_owners(mine, other, later):
    far = lax.axis_size("far")
    mine = mine + lax.ppermute(other, "core", [(0, 1), (1, 0)])
    total = mine[0]
    for ahead, hop in ((1, 1), (mine.shape[0] - 1, -1), (2, 2)):
        total = total + shift_near(mine[ahead], hop)
    total, _ = lax.optimization_barrier((total, later))
    total = total.reshape(far, -1, total.shape[1])
    return jnp.sum(lax.all_to_all(total, "far", 0, 0, tiled=True), axis=0)


def body(cotangent, spectrum, weights):
    space_count = lax.axis_size("space")
    _, channels, row_count, col_count = cotangent.shape
    local_modes, modes_y = spectrum.shape[0], spectrum.shape[3] // 2
    height, modes_x = row_count * space_count, local_modes * space_count
    block = lax.axis_index("space")

    partial = forward(cotangent[0], block, modes_x, modes_y, height)
    partial = lax.all_to_all(partial, "space", 0, 0, tiled=True)
    everyone, mine, other = middle(partial, weights, spectrum[:, 0])
    all_spec = lax.all_to_all(everyone, "space", 0, 0, tiled=True)
    grad_weights = sum_to_owners(mine, other, all_spec).reshape(local_modes, -1, 2 * modes_y)

    all_spec = all_spec.reshape(space_count, channels, local_modes, 2 * modes_y).transpose(1, 0, 2, 3)
    all_spec = all_spec.reshape(channels, modes_x, 2 * modes_y)
    grad_input = inverse(all_spec, block, row_count, col_count, height)
    return (grad_input[None], grad_weights)


def solution(mesh):
    dp_count, space_count = mesh.devices.shape
    chips = mesh.devices.reshape(FAR, dp_count // (2 * FAR), 2, space_count)
    return jax.shard_map(
        body,
        mesh=Mesh(chips, DP + ("space",)),
        in_specs=(P(DP, None, "space", None), P("space", DP, None, None), P("space", None, None, None)),
        out_specs=(P(DP, None, "space", None), P("space", DP, None)),
        check_vma=False,
    )
```

```python
import functools
import math

import jax
import jax.numpy as jnp
import ml_dtypes
import numpy as np
from jax import lax
from jax.experimental import pallas as pl
from jax.experimental.pallas import tpu as pltpu
from jax.sharding import Mesh
from jax.sharding import PartitionSpec as P

DP = ("far", "near", "core")
SPACE = ("row", "column")
FAR = 4
ROWS = 4
HOPS = (0, 1, 2, -1)
VMEM = pl.BlockSpec(memory_space=pltpu.VMEM)
HBM = pl.BlockSpec(memory_space=pltpu.HBM)
PARAMS = pltpu.CompilerParams(vmem_limit_bytes=24 << 20)


def halves(table):
    high = table.astype(ml_dtypes.bfloat16)
    low = (table - high.astype(np.float64)).astype(ml_dtypes.bfloat16)
    return high, low


def column_table(col_count, modes_y):
    phase = np.arange(col_count)[:, None] * np.arange(modes_y)[None, :] % col_count
    angles = phase * (2.0 * math.pi / col_count)
    return np.concatenate([np.cos(angles), -np.sin(angles)], axis=1)


def row_tables(modes_x, row_count, height):
    phase = np.arange(modes_x)[:, None] * np.arange(height)[None, :] % height
    angles = phase * (2.0 * math.pi / height)
    angles = angles.reshape(modes_x, height // row_count, row_count).transpose(1, 0, 2)
    return np.cos(angles), np.sin(angles)


def split(x):
    high = x.astype(jnp.bfloat16)
    return high, (x - high.astype(jnp.float32)).astype(jnp.bfloat16)


def dot(a, b):
    return jnp.dot(a, b, preferred_element_type=jnp.float32)


def first_half(x, modes_y):
    return lax.broadcasted_iota(jnp.int32, x.shape, x.ndim - 1) < modes_y


def mix(rows, spec, turned):
    high, low = zip(*map(split, spec))
    turned_high, turned_low = zip(*map(split, turned))

    def operand(c):
        return jnp.concatenate(
            [high[c], turned_high[c], low[c], turned_low[c], high[c], turned_high[c]], axis=0
        )

    out, width = [], spec[0].shape[1]
    for c in range(0, len(spec), 2):
        pair = dot(rows, jnp.concatenate([operand(c), operand(c + 1)], axis=1))
        out += [pair[:, :width], pair[:, width:]]
    return out


def forward_kernel(cot_hbm, basis_hbm, rows_hbm, out_ref, cot_ref, basis_ref, rows_ref, sems):
    channels, row_count, col_count = cot_ref.shape
    width, chunks = out_ref.shape[2], sems.shape[0] - 2
    step = channels // chunks
    copies = [
        pltpu.make_async_copy(basis_hbm, basis_ref, sems.at[chunks]),
        pltpu.make_async_copy(rows_hbm.at[lax.axis_index(SPACE)], rows_ref, sems.at[chunks + 1]),
    ]
    pieces = [slice(i * step, (i + 1) * step) for i in range(chunks)]
    loads = [
        pltpu.make_async_copy(cot_hbm.at[piece], cot_ref.at[piece], sems.at[i])
        for i, piece in enumerate(pieces)
    ]
    loads[0].start()
    for copy in copies + loads[1:]:
        copy.start()
    for copy in copies:
        copy.wait()
    for piece, load in zip(pieces, loads):
        load.wait()
        both = dot(cot_ref[piece].reshape(step * row_count, col_count), basis_ref[...])
        col_spec = both[:, :width] + both[:, width:]
        turned = pltpu.roll(col_spec, width // 2, 1)
        turned = jnp.where(first_half(turned, width // 2), turned, -turned)
        parts = [slice(c * row_count, (c + 1) * row_count) for c in range(step)]
        mixed = mix(rows_ref[...], [col_spec[p] for p in parts], [turned[p] for p in parts])
        for c, out in enumerate(mixed):
            out_ref[:, piece.start + c, :] = out


def forward(cotangent, modes_x, modes_y, height):
    channels, row_count, col_count = cotangent.shape
    basis = np.concatenate(halves(column_table(col_count, modes_y)), axis=1)
    table = np.concatenate(row_tables(modes_x, row_count, height), axis=2) / math.sqrt(height * col_count)
    high, low = halves(table)
    rows = np.concatenate([high, high, low], axis=2)
    chunks = 3
    return pl.pallas_call(
        forward_kernel,
        out_shape=jax.ShapeDtypeStruct((modes_x, channels, 2 * modes_y), jnp.float32),
        in_specs=[HBM, HBM, HBM],
        out_specs=VMEM,
        scratch_shapes=[
            pltpu.VMEM(cotangent.shape, jnp.bfloat16),
            pltpu.VMEM(basis.shape, jnp.bfloat16),
            pltpu.VMEM(rows.shape[1:], jnp.bfloat16),
            pltpu.SemaphoreType.DMA((chunks + 2,)),
        ],
        compiler_params=PARAMS,
        name="rows_to_modes",
    )(*(pltpu.with_memory_space_constraint(x, pltpu.HBM) for x in (cotangent, jnp.asarray(basis), jnp.asarray(rows))))


def inverse_kernel(spec_ref, rows_ref, basis_ref, out_ref):
    step, width = out_ref.shape[0], spec_ref.shape[2]
    first = pl.program_id(0) * step
    spec = [spec_ref[first + c] for c in range(step)]
    turned = [pltpu.roll(s, width // 2, 1) for s in spec]
    turned = [jnp.where(first_half(t, width // 2), -t, t) for t in turned]
    high, low = split(jnp.concatenate(mix(rows_ref[...], spec, turned), axis=0))
    raster = dot(jnp.concatenate([high, low, high], axis=1), basis_ref[...])
    out_ref[...] = raster.astype(out_ref.dtype).reshape(out_ref.shape)


def inverse(all_spec, block, row_count, col_count, height):
    channels, modes_x, width = all_spec.shape
    modes_y = width // 2
    high, low = halves(column_table(col_count, modes_y).T)
    basis = np.concatenate([high, high, low], axis=0)
    table = np.concatenate(row_tables(modes_x, row_count, height), axis=1) / math.sqrt(modes_x * modes_y)
    high, low = halves(table.transpose(0, 2, 1))
    rows = np.concatenate([high, high, low], axis=2)
    rows = lax.dynamic_index_in_dim(jnp.asarray(rows), block, 0, keepdims=False)
    step = 8
    return pl.pallas_call(
        inverse_kernel,
        grid=(channels // step,),
        out_shape=jax.ShapeDtypeStruct((channels, row_count, col_count), jnp.bfloat16),
        in_specs=[VMEM, VMEM, VMEM],
        out_specs=pl.BlockSpec((step, row_count, col_count), lambda i: (i, 0, 0)),
        compiler_params=PARAMS,
        name="modes_to_rows",
    )(all_spec, rows, jnp.asarray(basis))


def middle_kernel(got_ref, weights_ref, spectrum_ref, spec_ref, mine_ref, other_ref, one_ref, terms_ref):
    modes, channels, width = spectrum_ref.shape
    half = width // 2
    here, core = lax.axis_index("near"), lax.axis_index("core")
    grad = got_ref[pl.ds(0, modes)]
    for s in range(1, got_ref.shape[0] // modes):
        grad = grad + got_ref[pl.ds(s * modes, modes)]
    turned = pltpu.roll(grad, half, 2)

    for k in range(modes):
        straight, crossed = [], []
        for c in range(channels):
            weight = weights_ref[k, c]
            straight.append(jnp.sum(weight * grad[k], axis=0, keepdims=True))
            crossed.append(jnp.sum(weight * turned[k], axis=0, keepdims=True))
        straight = jnp.concatenate(straight, axis=0)
        crossed = jnp.concatenate(crossed, axis=0)
        left = first_half(straight, half)
        real_part = straight + pltpu.roll(straight, half, 1)
        imag_part = pltpu.roll(crossed, half, 1) - crossed
        one_ref[pl.ds(k, channels, stride=modes), :] = jnp.where(left, real_part, imag_part)
    one = one_ref[...]
    for s in range(spec_ref.shape[0]):
        spec_ref[s] = one

    for k in range(modes):
        own = spectrum_ref[k]
        left = first_half(own, half)
        flipped = pltpu.roll(own, half, 1)
        own_re = jnp.where(left, own, flipped)
        own_im = jnp.where(left, flipped, -own)
        for c in range(channels):
            terms_ref[pl.ds(c * channels * modes + k, channels, stride=modes), :] = (
                own_re[c : c + 1] * grad[k] + own_im[c : c + 1] * turned[k]
            )
    near, far, rows, _ = mine_ref.shape
    owned = channels * channels * modes // (2 * near * far)
    terms_ref[pl.ds(channels * channels * modes, 8), :] = jnp.zeros((8, width), jnp.float32)
    for ahead in range(near):
        column = lax.rem(here + HOPS[ahead] + near, near)
        for target in range(far):
            first = (target * near + column) * (2 * owned)
            zero = terms_ref[pl.ds(first, rows), :]
            one = terms_ref[pl.ds(first + owned, rows), :]
            mine_ref[ahead, target] = jnp.where(core == 0, zero, one)
            other_ref[ahead, target] = jnp.where(core == 0, one, zero)


def middle(got, weights, spectrum, copies):
    modes, channels, width = spectrum.shape
    near = lax.axis_size("near")
    far = lax.axis_size("far")
    rows = channels * channels * modes // (2 * near * far)
    terms = jax.ShapeDtypeStruct((near, far, pl.cdiv(rows, 8) * 8, width), jnp.float32)
    return pl.pallas_call(
        middle_kernel,
        out_shape=(jax.ShapeDtypeStruct((copies, channels * modes, width), jnp.float32), terms, terms),
        in_specs=[VMEM, VMEM, VMEM],
        out_specs=(VMEM, VMEM, VMEM),
        scratch_shapes=[
            pltpu.VMEM((channels * modes, width), jnp.float32),
            pltpu.VMEM((channels * channels * modes + 8, width), jnp.float32),
        ],
        compiler_params=PARAMS,
        name="modes",
    )(got, weights, spectrum)


def shift(x, hop):
    near, far = lax.axis_size("near"), lax.axis_size("far")
    chips = near * far
    return lax.ppermute(x, ("far", "near"), [(z, (z + hop) % chips) for z in range(chips)])


def sum_to_owners(mine, other, later):
    mine = mine + lax.ppermute(other, "core", [(0, 1), (1, 0)])
    total = mine[0]
    for ahead in range(1, mine.shape[0]):
        total = total + shift(mine[ahead], HOPS[ahead])
    total, _ = lax.optimization_barrier((total, later))
    return lax.all_to_all(total, "far", 0, 0, tiled=True)


def body(cotangent, spectrum, weights):
    space_count = lax.axis_size(SPACE)
    _, channels, row_count, col_count = cotangent.shape
    local_modes, modes_y = spectrum.shape[0], spectrum.shape[3] // 2
    height, modes_x = row_count * space_count, local_modes * space_count
    block = lax.axis_index(SPACE)

    partial = forward(cotangent[0], modes_x, modes_y, height)
    partial = lax.all_to_all(partial, "row", 0, 0, tiled=True)
    partial = jnp.sum(partial.reshape((lax.axis_size("row"), -1) + partial.shape[1:]), axis=0)
    partial = lax.all_to_all(partial, "column", 0, 0, tiled=True)
    everyone, mine, other = middle(partial, weights, spectrum[:, 0], space_count)
    all_spec = lax.all_to_all(everyone, SPACE, 0, 0, tiled=True)
    pairs = channels * channels // lax.axis_size(DP)
    terms = sum_to_owners(mine, other, all_spec)
    terms = terms.reshape(terms.shape[0], -1, local_modes, 2 * modes_y)[:, :pairs]
    grad_weights = jnp.sum(terms, axis=0).transpose(1, 0, 2)

    all_spec = all_spec.reshape(space_count, channels, local_modes, 2 * modes_y).transpose(1, 0, 2, 3)
    all_spec = all_spec.reshape(channels, modes_x, 2 * modes_y)
    grad_input = inverse(all_spec, block, row_count, col_count, height)
    return (grad_input[None], grad_weights)


def solution(mesh):
    dp_count, space_count = mesh.devices.shape
    chips = mesh.devices.reshape(FAR, dp_count // (2 * FAR), 2, ROWS, space_count // ROWS)
    return jax.shard_map(
        body,
        mesh=Mesh(chips, DP + SPACE),
        in_specs=(P(DP, None, SPACE, None), P(SPACE, DP, None, None), P(SPACE, None, None, None)),
        out_specs=(P(DP, None, SPACE, None), P(SPACE, DP, None)),
        check_vma=False,
    )
```

```python
import functools
import math

import jax
import jax.numpy as jnp
import ml_dtypes
import numpy as np
from jax import lax
from jax.experimental import pallas as pl
from jax.experimental.pallas import tpu as pltpu
from jax.sharding import Mesh
from jax.sharding import PartitionSpec as P

DP = ("far", "near", "core")
SPACE = ("row", "column")
FAR = 4
ROWS = 4
HOPS = (0, 1, 2, -1)
VMEM = pl.BlockSpec(memory_space=pltpu.VMEM)
HBM = pl.BlockSpec(memory_space=pltpu.HBM)
PARAMS = pltpu.CompilerParams(vmem_limit_bytes=24 << 20)


def halves(table):
    high = table.astype(ml_dtypes.bfloat16)
    low = (table - high.astype(np.float64)).astype(ml_dtypes.bfloat16)
    return high, low


def column_table(col_count, modes_y):
    phase = np.arange(col_count)[:, None] * np.arange(modes_y)[None, :] % col_count
    angles = phase * (2.0 * math.pi / col_count)
    return np.concatenate([np.cos(angles), -np.sin(angles)], axis=1)


def row_tables(modes_x, row_count, height):
    phase = np.arange(modes_x)[:, None] * np.arange(height)[None, :] % height
    angles = phase * (2.0 * math.pi / height)
    angles = angles.reshape(modes_x, height // row_count, row_count).transpose(1, 0, 2)
    return np.cos(angles), np.sin(angles)


def split(x):
    high = x.astype(jnp.bfloat16)
    return high, (x - high.astype(jnp.float32)).astype(jnp.bfloat16)


def dot(a, b):
    return jnp.dot(a, b, preferred_element_type=jnp.float32)


def first_half(x, modes_y):
    return lax.broadcasted_iota(jnp.int32, x.shape, x.ndim - 1) < modes_y


def mix(rows, spec, turned):
    high, low = zip(*map(split, spec))
    turned_high, turned_low = zip(*map(split, turned))

    def operand(c):
        return jnp.concatenate(
            [high[c], turned_high[c], low[c], turned_low[c], high[c], turned_high[c]], axis=0
        )

    out, width = [], spec[0].shape[1]
    for c in range(0, len(spec), 2):
        pair = dot(rows, jnp.concatenate([operand(c), operand(c + 1)], axis=1))
        out += [pair[:, :width], pair[:, width:]]
    return out


def forward_kernel(cot_hbm, basis_hbm, rows_hbm, out_ref, cot_ref, basis_ref, rows_ref, sems):
    channels, row_count, col_count = cot_ref.shape
    width, chunks = out_ref.shape[2], sems.shape[0] - 2
    step = channels // chunks
    copies = [
        pltpu.make_async_copy(basis_hbm, basis_ref, sems.at[chunks]),
        pltpu.make_async_copy(rows_hbm.at[lax.axis_index(SPACE)], rows_ref, sems.at[chunks + 1]),
    ]
    pieces = [slice(i * step, (i + 1) * step) for i in range(chunks)]
    loads = [
        pltpu.make_async_copy(cot_hbm.at[piece], cot_ref.at[piece], sems.at[i])
        for i, piece in enumerate(pieces)
    ]
    loads[0].start()
    for copy in copies + loads[1:]:
        copy.start()
    for copy in copies:
        copy.wait()
    for piece, load in zip(pieces, loads):
        load.wait()
        both = dot(cot_ref[piece].reshape(step * row_count, col_count), basis_ref[...])
        col_spec = both[:, :width] + both[:, width:]
        turned = pltpu.roll(col_spec, width // 2, 1)
        turned = jnp.where(first_half(turned, width // 2), turned, -turned)
        parts = [slice(c * row_count, (c + 1) * row_count) for c in range(step)]
        mixed = mix(rows_ref[...], [col_spec[p] for p in parts], [turned[p] for p in parts])
        for c, out in enumerate(mixed):
            out_ref[:, piece.start + c, :] = out


def forward(cotangent, modes_x, modes_y, height):
    channels, row_count, col_count = cotangent.shape
    basis = np.concatenate(halves(column_table(col_count, modes_y)), axis=1)
    table = np.concatenate(row_tables(modes_x, row_count, height), axis=2) / math.sqrt(height * col_count)
    high, low = halves(table)
    rows = np.concatenate([high, high, low], axis=2)
    chunks = 1
    return pl.pallas_call(
        forward_kernel,
        out_shape=jax.ShapeDtypeStruct((modes_x, channels, 2 * modes_y), jnp.float32),
        in_specs=[HBM, HBM, HBM],
        out_specs=VMEM,
        scratch_shapes=[
            pltpu.VMEM(cotangent.shape, jnp.bfloat16),
            pltpu.VMEM(basis.shape, jnp.bfloat16),
            pltpu.VMEM(rows.shape[1:], jnp.bfloat16),
            pltpu.SemaphoreType.DMA((chunks + 2,)),
        ],
        compiler_params=PARAMS,
        name="rows_to_modes",
    )(*(pltpu.with_memory_space_constraint(x, pltpu.HBM) for x in (cotangent, jnp.asarray(basis), jnp.asarray(rows))))


def inverse_kernel(spec_ref, rows_ref, basis_ref, out_ref):
    step, width = out_ref.shape[0], spec_ref.shape[2]
    first = pl.program_id(0) * step
    spec = [spec_ref[first + c] for c in range(step)]
    turned = [pltpu.roll(s, width // 2, 1) for s in spec]
    turned = [jnp.where(first_half(t, width // 2), -t, t) for t in turned]
    high, low = split(jnp.concatenate(mix(rows_ref[...], spec, turned), axis=0))
    raster = dot(jnp.concatenate([high, low, high], axis=1), basis_ref[...])
    out_ref[...] = raster.astype(out_ref.dtype).reshape(out_ref.shape)


def inverse(all_spec, block, row_count, col_count, height):
    channels, modes_x, width = all_spec.shape
    modes_y = width // 2
    high, low = halves(column_table(col_count, modes_y).T)
    basis = np.concatenate([high, high, low], axis=0)
    table = np.concatenate(row_tables(modes_x, row_count, height), axis=1) / math.sqrt(modes_x * modes_y)
    high, low = halves(table.transpose(0, 2, 1))
    rows = np.concatenate([high, high, low], axis=2)
    rows = lax.dynamic_index_in_dim(jnp.asarray(rows), block, 0, keepdims=False)
    step = 8
    return pl.pallas_call(
        inverse_kernel,
        grid=(channels // step,),
        out_shape=jax.ShapeDtypeStruct((channels, row_count, col_count), jnp.bfloat16),
        in_specs=[VMEM, VMEM, VMEM],
        out_specs=pl.BlockSpec((step, row_count, col_count), lambda i: (i, 0, 0)),
        compiler_params=PARAMS,
        name="modes_to_rows",
    )(all_spec, rows, jnp.asarray(basis))


def middle_kernel(got_ref, weights_ref, spectrum_ref, spec_ref, mine_ref, other_ref, one_ref, terms_ref):
    modes, channels, width = spectrum_ref.shape
    half = width // 2
    here, core = lax.axis_index("near"), lax.axis_index("core")
    grad = got_ref[pl.ds(0, modes)]
    for s in range(1, got_ref.shape[0] // modes):
        grad = grad + got_ref[pl.ds(s * modes, modes)]
    turned = pltpu.roll(grad, half, 2)

    for k in range(modes):
        straight, crossed = [], []
        for c in range(channels):
            weight = weights_ref[k, c]
            straight.append(jnp.sum(weight * grad[k], axis=0, keepdims=True))
            crossed.append(jnp.sum(weight * turned[k], axis=0, keepdims=True))
        straight = jnp.concatenate(straight, axis=0)
        crossed = jnp.concatenate(crossed, axis=0)
        left = first_half(straight, half)
        real_part = straight + pltpu.roll(straight, half, 1)
        imag_part = pltpu.roll(crossed, half, 1) - crossed
        one_ref[pl.ds(k, channels, stride=modes), :] = jnp.where(left, real_part, imag_part)
    one = one_ref[...]
    for s in range(spec_ref.shape[0]):
        spec_ref[s] = one

    for k in range(modes):
        own = spectrum_ref[k]
        left = first_half(own, half)
        flipped = pltpu.roll(own, half, 1)
        own_re = jnp.where(left, own, flipped)
        own_im = jnp.where(left, flipped, -own)
        for c in range(channels):
            terms_ref[pl.ds(c * channels * modes + k, channels, stride=modes), :] = (
                own_re[c : c + 1] * grad[k] + own_im[c : c + 1] * turned[k]
            )
    near, far, rows, _ = mine_ref.shape
    owned = channels * channels * modes // (2 * near * far)
    terms_ref[pl.ds(channels * channels * modes, 8), :] = jnp.zeros((8, width), jnp.float32)
    for ahead in range(near):
        column = lax.rem(here + HOPS[ahead] + near, near)
        for target in range(far):
            first = (target * near + column) * (2 * owned)
            zero = terms_ref[pl.ds(first, rows), :]
            one = terms_ref[pl.ds(first + owned, rows), :]
            mine_ref[ahead, target] = jnp.where(core == 0, zero, one)
            other_ref[ahead, target] = jnp.where(core == 0, one, zero)


def middle(got, weights, spectrum, copies):
    modes, channels, width = spectrum.shape
    near = lax.axis_size("near")
    far = lax.axis_size("far")
    rows = channels * channels * modes // (2 * near * far)
    terms = jax.ShapeDtypeStruct((near, far, pl.cdiv(rows, 8) * 8, width), jnp.float32)
    return pl.pallas_call(
        middle_kernel,
        out_shape=(jax.ShapeDtypeStruct((copies, channels * modes, width), jnp.float32), terms, terms),
        in_specs=[VMEM, VMEM, VMEM],
        out_specs=(VMEM, VMEM, VMEM),
        scratch_shapes=[
            pltpu.VMEM((channels * modes, width), jnp.float32),
            pltpu.VMEM((channels * channels * modes + 8, width), jnp.float32),
        ],
        compiler_params=PARAMS,
        name="modes",
    )(got, weights, spectrum)


def shift(x, hop):
    near, far = lax.axis_size("near"), lax.axis_size("far")
    chips = near * far
    return lax.ppermute(x, ("far", "near"), [(z, (z + hop) % chips) for z in range(chips)])


def sum_to_owners(mine, other, later):
    mine = mine + lax.ppermute(other, "core", [(0, 1), (1, 0)])
    total = mine[0]
    for ahead in (2, 1, 3):
        total = total + shift(mine[ahead], HOPS[ahead])
    total, _ = lax.optimization_barrier((total, later))
    return lax.all_to_all(total, "far", 0, 0, tiled=True)


def body(cotangent, spectrum, weights):
    space_count = lax.axis_size(SPACE)
    _, channels, row_count, col_count = cotangent.shape
    local_modes, modes_y = spectrum.shape[0], spectrum.shape[3] // 2
    height, modes_x = row_count * space_count, local_modes * space_count
    block = lax.axis_index(SPACE)

    partial = forward(cotangent[0], modes_x, modes_y, height)
    partial = lax.all_to_all(partial, "row", 0, 0, tiled=True)
    partial = jnp.sum(partial.reshape((lax.axis_size("row"), -1) + partial.shape[1:]), axis=0)
    partial = lax.all_to_all(partial, "column", 0, 0, tiled=True)
    everyone, mine, other = middle(partial, weights, spectrum[:, 0], space_count)
    all_spec = lax.all_to_all(everyone, SPACE, 0, 0, tiled=True)
    pairs = channels * channels // lax.axis_size(DP)
    terms = sum_to_owners(mine, other, all_spec)
    terms = terms.reshape(terms.shape[0], -1, local_modes, 2 * modes_y)[:, :pairs]
    grad_weights = jnp.sum(terms, axis=0).transpose(1, 0, 2)

    all_spec = all_spec.reshape(space_count, channels, local_modes, 2 * modes_y).transpose(1, 0, 2, 3)
    all_spec = all_spec.reshape(channels, modes_x, 2 * modes_y)
    grad_input = inverse(all_spec, block, row_count, col_count, height)
    return (grad_input[None], grad_weights)


def solution(mesh):
    dp_count, space_count = mesh.devices.shape
    chips = mesh.devices.reshape(FAR, dp_count // (2 * FAR), 2, ROWS, space_count // ROWS)
    return jax.shard_map(
        body,
        mesh=Mesh(chips, DP + SPACE),
        in_specs=(P(DP, None, SPACE, None), P(SPACE, DP, None, None), P(SPACE, None, None, None)),
        out_specs=(P(DP, None, SPACE, None), P(SPACE, DP, None)),
        check_vma=False,
    )
```

```python
import functools
import math

import jax
import jax.numpy as jnp
import ml_dtypes
import numpy as np
from jax import lax
from jax.experimental import pallas as pl
from jax.experimental.pallas import tpu as pltpu
from jax.sharding import Mesh
from jax.sharding import PartitionSpec as P

DP = ("far", "near", "core")
SPACE = ("row", "column")
FAR = 4
ROWS = 4
SENDS = 4
HOPS = (0, 1, 2, -1)
VMEM = pl.BlockSpec(memory_space=pltpu.VMEM)
HBM = pl.BlockSpec(memory_space=pltpu.HBM)
PARAMS = pltpu.CompilerParams(vmem_limit_bytes=24 << 20)


def halves(table):
    high = table.astype(ml_dtypes.bfloat16)
    low = (table - high.astype(np.float64)).astype(ml_dtypes.bfloat16)
    return high, low


def column_table(col_count, modes_y):
    phase = np.arange(col_count)[:, None] * np.arange(modes_y)[None, :] % col_count
    angles = phase * (2.0 * math.pi / col_count)
    return np.concatenate([np.cos(angles), -np.sin(angles)], axis=1)


def row_tables(modes_x, row_count, height):
    phase = np.arange(modes_x)[:, None] * np.arange(height)[None, :] % height
    angles = phase * (2.0 * math.pi / height)
    angles = angles.reshape(modes_x, height // row_count, row_count).transpose(1, 0, 2)
    return np.cos(angles), np.sin(angles)


def split(x):
    high = x.astype(jnp.bfloat16)
    return high, (x - high.astype(jnp.float32)).astype(jnp.bfloat16)


def dot(a, b):
    return jnp.dot(a, b, preferred_element_type=jnp.float32)


def first_half(x, modes_y):
    return lax.broadcasted_iota(jnp.int32, x.shape, x.ndim - 1) < modes_y


def mix(rows, spec, turned):
    high, low = zip(*map(split, spec))
    turned_high, turned_low = zip(*map(split, turned))

    def operand(c):
        return jnp.concatenate(
            [high[c], turned_high[c], low[c], turned_low[c], high[c], turned_high[c]], axis=0
        )

    out, width = [], spec[0].shape[1]
    for c in range(0, len(spec), 2):
        pair = dot(rows, jnp.concatenate([operand(c), operand(c + 1)], axis=1))
        out += [pair[:, :width], pair[:, width:]]
    return out


def forward_kernel(cot_hbm, basis_hbm, rows_hbm, out_ref, cot_ref, basis_ref, rows_ref, sems):
    channels, row_count, col_count = cot_ref.shape
    width, chunks = out_ref.shape[2], sems.shape[0] - 2
    step = channels // chunks
    copies = [
        pltpu.make_async_copy(basis_hbm, basis_ref, sems.at[chunks]),
        pltpu.make_async_copy(rows_hbm.at[lax.axis_index(SPACE)], rows_ref, sems.at[chunks + 1]),
    ]
    pieces = [slice(i * step, (i + 1) * step) for i in range(chunks)]
    loads = [
        pltpu.make_async_copy(cot_hbm.at[piece], cot_ref.at[piece], sems.at[i])
        for i, piece in enumerate(pieces)
    ]
    loads[0].start()
    for copy in copies + loads[1:]:
        copy.start()
    for copy in copies:
        copy.wait()
    for piece, load in zip(pieces, loads):
        load.wait()
        both = dot(cot_ref[piece].reshape(step * row_count, col_count), basis_ref[...])
        col_spec = both[:, :width] + both[:, width:]
        turned = pltpu.roll(col_spec, width // 2, 1)
        turned = jnp.where(first_half(turned, width // 2), turned, -turned)
        parts = [slice(c * row_count, (c + 1) * row_count) for c in range(step)]
        mixed = mix(rows_ref[...], [col_spec[p] for p in parts], [turned[p] for p in parts])
        for c, out in enumerate(mixed):
            out_ref[:, piece.start + c, :] = out


def forward(cotangent, modes_x, modes_y, height):
    channels, row_count, col_count = cotangent.shape
    basis = np.concatenate(halves(column_table(col_count, modes_y)), axis=1)
    table = np.concatenate(row_tables(modes_x, row_count, height), axis=2) / math.sqrt(height * col_count)
    high, low = halves(table)
    rows = np.concatenate([high, high, low], axis=2)
    chunks = 1
    return pl.pallas_call(
        forward_kernel,
        out_shape=jax.ShapeDtypeStruct((modes_x, channels, 2 * modes_y), jnp.float32),
        in_specs=[HBM, HBM, HBM],
        out_specs=VMEM,
        scratch_shapes=[
            pltpu.VMEM(cotangent.shape, jnp.bfloat16),
            pltpu.VMEM(basis.shape, jnp.bfloat16),
            pltpu.VMEM(rows.shape[1:], jnp.bfloat16),
            pltpu.SemaphoreType.DMA((chunks + 2,)),
        ],
        compiler_params=PARAMS,
        name="rows_to_modes",
    )(*(pltpu.with_memory_space_constraint(x, pltpu.HBM) for x in (cotangent, jnp.asarray(basis), jnp.asarray(rows))))


def inverse_kernel(spec_ref, rows_ref, basis_ref, out_ref):
    step, width = out_ref.shape[0], spec_ref.shape[2]
    first = pl.program_id(0) * step
    spec = [spec_ref[first + c] for c in range(step)]
    turned = [pltpu.roll(s, width // 2, 1) for s in spec]
    turned = [jnp.where(first_half(t, width // 2), -t, t) for t in turned]
    high, low = split(jnp.concatenate(mix(rows_ref[...], spec, turned), axis=0))
    raster = dot(jnp.concatenate([high, low, high], axis=1), basis_ref[...])
    out_ref[...] = raster.astype(out_ref.dtype).reshape(out_ref.shape)


def inverse(all_spec, block, row_count, col_count, height):
    channels, modes_x, width = all_spec.shape
    modes_y = width // 2
    high, low = halves(column_table(col_count, modes_y).T)
    basis = np.concatenate([high, high, low], axis=0)
    table = np.concatenate(row_tables(modes_x, row_count, height), axis=1) / math.sqrt(modes_x * modes_y)
    high, low = halves(table.transpose(0, 2, 1))
    rows = np.concatenate([high, high, low], axis=2)
    rows = lax.dynamic_index_in_dim(jnp.asarray(rows), block, 0, keepdims=False)
    step = 8
    return pl.pallas_call(
        inverse_kernel,
        grid=(channels // step,),
        out_shape=jax.ShapeDtypeStruct((channels, row_count, col_count), jnp.bfloat16),
        in_specs=[VMEM, VMEM, VMEM],
        out_specs=pl.BlockSpec((step, row_count, col_count), lambda i: (i, 0, 0)),
        compiler_params=PARAMS,
        name="modes_to_rows",
    )(all_spec, rows, jnp.asarray(basis))


def middle_kernel(got_ref, weights_ref, spectrum_ref, spec_hbm, mine_ref, other_ref, one_ref, copies_ref, terms_ref, sems):
    modes, channels, width = spectrum_ref.shape
    half = width // 2
    here, core = lax.axis_index("near"), lax.axis_index("core")
    grad = got_ref[pl.ds(0, modes)]
    for s in range(1, got_ref.shape[0] // modes):
        grad = grad + got_ref[pl.ds(s * modes, modes)]
    turned = pltpu.roll(grad, half, 2)

    for k in range(modes):
        straight, crossed = [], []
        for c in range(channels):
            weight = weights_ref[k, c]
            straight.append(jnp.sum(weight * grad[k], axis=0, keepdims=True))
            crossed.append(jnp.sum(weight * turned[k], axis=0, keepdims=True))
        straight = jnp.concatenate(straight, axis=0)
        crossed = jnp.concatenate(crossed, axis=0)
        left = first_half(straight, half)
        real_part = straight + pltpu.roll(straight, half, 1)
        imag_part = pltpu.roll(crossed, half, 1) - crossed
        one_ref[pl.ds(k, channels, stride=modes), :] = jnp.where(left, real_part, imag_part)
    one = one_ref[...]
    batch = copies_ref.shape[0]
    for s in range(batch):
        copies_ref[s] = one
    sends = [
        pltpu.make_async_copy(copies_ref, spec_hbm.at[pl.ds(i * batch, batch)], sems.at[i])
        for i in range(sems.shape[0])
    ]
    for send in sends:
        send.start()

    for k in range(modes):
        own = spectrum_ref[k]
        left = first_half(own, half)
        flipped = pltpu.roll(own, half, 1)
        own_re = jnp.where(left, own, flipped)
        own_im = jnp.where(left, flipped, -own)
        for c in range(channels):
            terms_ref[pl.ds(c * channels * modes + k, channels, stride=modes), :] = (
                own_re[c : c + 1] * grad[k] + own_im[c : c + 1] * turned[k]
            )
    near, far, rows, _ = mine_ref.shape
    owned = channels * channels * modes // (2 * near * far)
    terms_ref[pl.ds(channels * channels * modes, 8), :] = jnp.zeros((8, width), jnp.float32)
    for ahead in range(near):
        column = lax.rem(here + HOPS[ahead] + near, near)
        for target in range(far):
            first = (target * near + column) * (2 * owned)
            zero = terms_ref[pl.ds(first, rows), :]
            one = terms_ref[pl.ds(first + owned, rows), :]
            mine_ref[ahead, target] = jnp.where(core == 0, zero, one)
            other_ref[ahead, target] = jnp.where(core == 0, one, zero)
    for send in sends:
        send.wait()


def middle(got, weights, spectrum, copies):
    modes, channels, width = spectrum.shape
    near = lax.axis_size("near")
    far = lax.axis_size("far")
    rows = channels * channels * modes // (2 * near * far)
    terms = jax.ShapeDtypeStruct((near, far, pl.cdiv(rows, 8) * 8, width), jnp.float32)
    return pl.pallas_call(
        middle_kernel,
        out_shape=(jax.ShapeDtypeStruct((copies, channels * modes, width), jnp.float32), terms, terms),
        in_specs=[VMEM, VMEM, VMEM],
        out_specs=(HBM, VMEM, VMEM),
        scratch_shapes=[
            pltpu.VMEM((channels * modes, width), jnp.float32),
            pltpu.VMEM((copies // SENDS, channels * modes, width), jnp.float32),
            pltpu.VMEM((channels * channels * modes + 8, width), jnp.float32),
            pltpu.SemaphoreType.DMA((SENDS,)),
        ],
        compiler_params=PARAMS,
        name="modes",
    )(got, weights, spectrum)


def shift(x, hop):
    near, far = lax.axis_size("near"), lax.axis_size("far")
    chips = near * far
    return lax.ppermute(x, ("far", "near"), [(z, (z + hop) % chips) for z in range(chips)])


def sum_to_owners(mine, other, later):
    mine = mine + lax.ppermute(other, "core", [(0, 1), (1, 0)])
    total = mine[0]
    for ahead in (2, 1, 3):
        total = total + shift(mine[ahead], HOPS[ahead])
    total, _ = lax.optimization_barrier((total, later))
    return lax.all_to_all(total, "far", 0, 0, tiled=True)


def body(cotangent, spectrum, weights):
    space_count = lax.axis_size(SPACE)
    _, channels, row_count, col_count = cotangent.shape
    local_modes, modes_y = spectrum.shape[0], spectrum.shape[3] // 2
    height, modes_x = row_count * space_count, local_modes * space_count
    block = lax.axis_index(SPACE)

    partial = forward(cotangent[0], modes_x, modes_y, height)
    partial = lax.all_to_all(partial, "row", 0, 0, tiled=True)
    partial = jnp.sum(partial.reshape((lax.axis_size("row"), -1) + partial.shape[1:]), axis=0)
    partial = lax.all_to_all(partial, "column", 0, 0, tiled=True)
    everyone, mine, other = middle(partial, weights, spectrum[:, 0], space_count)
    all_spec = lax.all_to_all(everyone, SPACE, 0, 0, tiled=True)
    pairs = channels * channels // lax.axis_size(DP)
    terms = sum_to_owners(mine, other, all_spec)
    terms = terms.reshape(terms.shape[0], -1, local_modes, 2 * modes_y)[:, :pairs]
    grad_weights = jnp.sum(terms, axis=0).transpose(1, 0, 2)

    all_spec = all_spec.reshape(space_count, channels, local_modes, 2 * modes_y).transpose(1, 0, 2, 3)
    all_spec = all_spec.reshape(channels, modes_x, 2 * modes_y)
    grad_input = inverse(all_spec, block, row_count, col_count, height)
    return (grad_input[None], grad_weights)


def solution(mesh):
    dp_count, space_count = mesh.devices.shape
    chips = mesh.devices.reshape(FAR, dp_count // (2 * FAR), 2, ROWS, space_count // ROWS)
    return jax.shard_map(
        body,
        mesh=Mesh(chips, DP + SPACE),
        in_specs=(P(DP, None, SPACE, None), P(SPACE, DP, None, None), P(SPACE, None, None, None)),
        out_specs=(P(DP, None, SPACE, None), P(SPACE, DP, None)),
        check_vma=False,
    )
```
